256 devices in a mesh: col: 64 (over x, z, core), row: 4 (over y).
Axes of the slice: x: 4, y: 4, z: 8, core: 2. Of those that a mesh axis runs over, the one named last changes fastest.
Arguments:
- grad_t: float32 [56, 512, 8192], P(None, 'col', 'row'), may hold values from -6 to 6
- coupling: float32 [56, 512, 3, 512], P(None, 'col', None, 'row'), may hold values from -0.15625 to 0.15625
- diag_inverse: float32 [3, 512, 512], replicated, as said below
Outputs:
- updated: float32 [56, 512, 8192], P(None, 'col', 'row')
The draws below stay inside these ranges and needn't reach their ends.
Inputs may be any that keep to these rules, and one draw needn't show every extreme that they name: `diag_inverse`: upper triangular; diagonal entries between 0.5 and 2.
All inputs are finite; a program needn't handle non-finite values.
Results may differ from the reference program's by a relative error of at most 0.0001.
Values sent between devices are 32-bit elements; how exact they have to be, the bound alone decides.
No kernel may reach another device: no remote copies, remote signals or barrier semaphores. Data moves between devices by JAX's collectives and lax.ppermute only.
A program may use at most 128 MiB of HBM per device.

```python
import math
import jax
import jax.numpy as jnp
from jax import lax

MODEL_WIDTH = 8192
PANEL_WIDTH = 512
PANELS = 3
CYCLES = 56


def draw_diag_inverse(key, part):
    key_off, key_diag = jax.random.split(jax.random.fold_in(key, 11))
    off_part = jax.random.normal(key_off, (PANELS, PANEL_WIDTH, PANEL_WIDTH), jnp.float32) * (0.6 / math.sqrt(PANEL_WIDTH))
    upper = jnp.triu(jnp.ones((PANEL_WIDTH, PANEL_WIDTH), jnp.float32), 1)
    diagonal = jnp.exp(jax.random.uniform(key_diag, (PANELS, PANEL_WIDTH), jnp.float32, math.log(0.5), math.log(2.0)))
    return off_part * upper + diagonal[:, :, None] * jnp.eye(PANEL_WIDTH, dtype=jnp.float32)


def shard_levels(own_key, shape, pieces, smallest, largest):
    level, own = 1.0, jax.random.fold_in(own_key, 6)
    for dim, shards_of in pieces:
        heights = jnp.exp(jax.random.uniform(jax.random.fold_in(own, dim), (shards_of,), jnp.float32, smallest / len(pieces), largest / len(pieces)))
        level = level * jnp.repeat(heights, shape[dim] // shards_of).reshape([-1 if axis == dim else 1 for axis in range(len(shape))])
    return level


def bell_draw(stream_key, shape, width, most, cuts=(), kind=jnp.bfloat16):
    result = width * jax.random.normal(stream_key, shape, jnp.float32)
    if cuts:
        result = result * shard_levels(stream_key, shape, cuts, -0.22, 0.18)
    return jnp.clip(result, -most, most).astype(kind)


def setup_inputs(seed: int = 0) -> dict:
    arg_keys = jax.random.split(jax.random.key(seed), 4)
    grad_t = bell_draw(arg_keys[0], (CYCLES, PANEL_WIDTH, MODEL_WIDTH), 1.0, 6.0, ((1, 64), (2, 4)), jnp.float32)
    coupling = bell_draw(arg_keys[1], (CYCLES, PANEL_WIDTH, PANELS, PANEL_WIDTH), (PANELS * PANEL_WIDTH) ** -0.5, 0.15625, ((1, 64), (3, 4)), jnp.float32)
    diag_inverse = draw_diag_inverse(jax.random.fold_in(arg_keys[3], 71), 0)
    return {"grad_t": grad_t, "coupling": coupling, "diag_inverse": diag_inverse}


def reference(grad_t, coupling, diag_inverse):
    trailing = grad_t
    solved_list = []
    for panel_step in range(PANELS):
        solution = jnp.dot(diag_inverse[panel_step].T, trailing[0], precision=lax.Precision.HIGHEST, preferred_element_type=jnp.float32)
        solved_list.append(solution)
        coupled = coupling[panel_step + 1:, :, panel_step, :]
        flat_rows = coupled.reshape(-1, PANEL_WIDTH)
        update = jnp.dot(flat_rows, solution, precision=lax.Precision.HIGHEST, preferred_element_type=jnp.float32)
        trailing = trailing[1:] - update.reshape(coupled.shape[0], PANEL_WIDTH, -1)
    return jnp.concatenate([jnp.stack(solved_list), trailing], axis=0)
```

```python
import jax
import jax.numpy as jnp
from jax import lax
from jax.sharding import PartitionSpec as P

PANELS = 3


def dot(left, right, contract, precision=lax.Precision.HIGHEST):
    return lax.dot_general(
        left, right, (contract, ((), ())), precision=precision, preferred_element_type=jnp.float32
    )


def body(grad_t, coupling, diag_inverse):
    cycles, local_rows, columns = grad_t.shape
    width = diag_inverse.shape[1]
    own_first = lax.axis_index("col") * local_rows
    inner = jnp.stack([coupling[1, :, 0], coupling[2, :, 0], coupling[2, :, 1]])
    inner = lax.all_gather(inner, "row", axis=2, tiled=True)
    folded = jnp.stack(
        [dot(inner[n], diag_inverse[k], ((1,), (1,))) for n, k in enumerate((0, 0, 1))]
    )
    payload = jnp.concatenate([grad_t[:PANELS], folded], axis=2)
    whole = lax.all_gather(payload, "col", axis=1, tiled=True)
    u10, u20, u21 = (whole[n, :, columns:] for n in range(3))

    left = []
    for k in range(PANELS):
        coupled = lax.all_gather(coupling[PANELS:, :, k, :], "row", axis=2, tiled=True)
        part = dot(coupled.reshape(-1, width), diag_inverse[k], ((1,), (1,)))
        own = lax.dynamic_slice_in_dim(diag_inverse[k], own_first, local_rows, 1).T
        tops = [jnp.zeros((local_rows, width), jnp.float32) for _ in range(PANELS)]
        tops[k] = -own
        left.append(jnp.concatenate(tops + [part], axis=0))
    m2 = left[2]
    m1 = left[1] - dot(m2, u21, ((1,), (0,)))
    m0 = left[0] - dot(m2, u20, ((1,), (0,))) - dot(m1, u10, ((1,), (0,)))
    m = jnp.concatenate([m0, m1, m2], axis=1)
    panels = whole[:, :, :columns].reshape(PANELS * width, columns)
    product = dot(m, panels, ((1,), (0,)), lax.Precision.HIGH).reshape(grad_t.shape)
    base = jnp.where(jnp.arange(cycles)[:, None, None] < PANELS, 0.0, grad_t)
    return base - product


def solution(mesh):
    in_specs = (P(None, "col", "row"), P(None, "col", None, "row"), P())
    out_specs = P(None, "col", "row")
    return jax.shard_map(body, mesh=mesh, in_specs=in_specs, out_specs=out_specs, check_vma=False)
```

```python
import jax
import jax.numpy as jnp
from jax import lax
from jax.sharding import PartitionSpec as P


PANELS = 3


def dot(left, right, contract, precision=lax.Precision.HIGH):
    return lax.dot_general(
        left, right, (contract, ((), ())), precision=precision, preferred_element_type=jnp.float32
    )


def from_ahead(value, axis, size, steps):
    return lax.ppermute(value, axis, [(i, (i - steps) % size) for i in range(size)])


def body(rows, cols, grad_t, coupling, diag_inverse):
    cycles, local_rows, columns = grad_t.shape
    width = diag_inverse.shape[1]
    piece = coupling.shape[3]
    me_col, me_row = lax.axis_index("col"), lax.axis_index("row")
    core = me_col % 2
    own_first = me_col * local_rows
    partner = [(i, i ^ 1) for i in range(cols)]

    panels = lax.all_gather(grad_t[:PANELS], "col", axis=1, tiled=True)

    coupled = coupling[PANELS:].transpose(2, 0, 1, 3).reshape(PANELS, -1, piece)
    slot_list = [coupled]
    for r in range(1, rows):
        slot_list.append(from_ahead(coupled, "row", rows, r))
    coupled = jnp.concatenate(slot_list, axis=2)

    inner = jnp.stack([coupling[1, :, 0], coupling[2, :, 0], coupling[2, :, 1]])
    inner = lax.all_gather(inner, "col")
    half = lax.dynamic_slice_in_dim(inner, core * (cols // 2), cols // 2, 0)
    near = [half, from_ahead(half, "row", rows, 1), from_ahead(half, "row", rows, rows - 1)]
    cut = cols // 4
    far = jnp.concatenate(
        [
            from_ahead(near[1][:cut], "row", rows, 1),
            from_ahead(near[2][cut:], "row", rows, rows - 1),
        ],
        axis=0,
    )
    half = jnp.concatenate([near[0], near[1], far, near[2]], axis=3)
    other = lax.ppermute(half, "col", partner)
    inner = jnp.concatenate(
        [jnp.where(core == 0, half, other), jnp.where(core == 0, other, half)], axis=0
    )
    c10, c20, c21 = (inner[:, n].reshape(width, width) for n in range(3))

    slots = diag_inverse.reshape(PANELS, width, rows, piece)
    slots = lax.dynamic_slice_in_dim(
        jnp.concatenate([slots, slots], axis=2), me_row, rows, 2
    ).reshape(PANELS, width, width)

    left = []
    for k in range(PANELS):
        part = dot(coupled[k], slots[k], ((1,), (1,)))
        own = lax.dynamic_slice_in_dim(diag_inverse[k], own_first, local_rows, 1).T
        tops = [jnp.zeros((local_rows, width), jnp.float32) for _ in range(PANELS)]
        tops[k] = -own
        left.append(jnp.concatenate(tops + [part], axis=0))
    u10 = dot(c10, slots[0], ((1,), (1,)))
    u20 = dot(c20, slots[0], ((1,), (1,)))
    u21 = dot(c21, slots[1], ((1,), (1,)))
    m2 = left[2]
    m1 = left[1] - dot(m2, u21, ((1,), (0,)))
    m0 = left[0] - dot(m2, u20, ((1,), (0,))) - dot(m1, u10, ((1,), (0,)))
    m = jnp.concatenate([m0, m1, m2], axis=1)
    product = dot(m, panels.reshape(PANELS * width, columns), ((1,), (0,)))
    base = jnp.where(jnp.arange(cycles)[:, None, None] < PANELS, 0.0, grad_t)
    return base - product.reshape(grad_t.shape)


def solution(mesh):
    in_specs = (P(None, "col", "row"), P(None, "col", None, "row"), P())
    out_specs = P(None, "col", "row")
    rows, cols = mesh.shape["row"], mesh.shape["col"]

    def step(*args):
        return body(rows, cols, *args)

    return jax.shard_map(step, mesh=mesh, in_specs=in_specs, out_specs=out_specs, check_vma=False)
```

```python
import jax
import jax.numpy as jnp
from jax import lax
from jax.sharding import PartitionSpec as P

PANELS = 3


def dot(left, right, contract, precision=lax.Precision.HIGH):
    return lax.dot_general(
        left, right, (contract, ((), ())), precision=precision, preferred_element_type=jnp.float32
    )


def from_ahead(value, axis, size, steps):
    return lax.ppermute(value, axis, [(i, (i - steps) % size) for i in range(size)])


def body(rows, cols, grad_t, coupling, diag_inverse):
    cycles, local_rows, columns = grad_t.shape
    width = diag_inverse.shape[1]
    piece = coupling.shape[3]
    me_col, me_row = lax.axis_index("col"), lax.axis_index("row")
    core = me_col % 2
    own_first = me_col * local_rows
    partner = [(i, i ^ 1) for i in range(cols)]

    panels = lax.all_gather(grad_t[:PANELS], "col", axis=1, tiled=True)

    coupled = coupling[PANELS:].transpose(2, 0, 1, 3).reshape(PANELS, -1, piece)
    slot_list = [coupled]
    for r in range(1, rows):
        slot_list.append(from_ahead(coupled, "row", rows, r))
    coupled = jnp.concatenate(slot_list, axis=2)

    chips = cols // 2
    inner = jnp.stack([coupling[1, :, 0], coupling[2, :, 0], coupling[2, :, 1]])
    same_core = [[2 * chip + c for chip in range(chips)] for c in range(2)]
    copies = jnp.broadcast_to(inner[None], (chips,) + inner.shape)
    half = lax.all_to_all(copies, "col", 0, 0, axis_index_groups=same_core)
    near = [from_ahead(half, "row", rows, 1), from_ahead(half, "row", rows, rows - 1)]
    cut = chips // 2
    far = jnp.concatenate(
        [
            from_ahead(near[0][:cut], "row", rows, 1),
            from_ahead(near[1][cut:], "row", rows, rows - 1),
        ],
        axis=0,
    )
    half = jnp.concatenate([half, near[0], far, near[1]], axis=3)
    other = lax.ppermute(half, "col", partner)
    first, second = jnp.where(core == 0, half, other), jnp.where(core == 0, other, half)
    inner = jnp.stack([first, second], axis=1)
    c10, c20, c21 = (inner[:, :, n].reshape(width, width) for n in range(3))

    slots = diag_inverse.reshape(PANELS, width, rows, piece)
    slots = lax.dynamic_slice_in_dim(
        jnp.concatenate([slots, slots], axis=2), me_row, rows, 2
    ).reshape(PANELS, width, width)

    left = []
    for k in range(PANELS):
        part = dot(coupled[k], slots[k], ((1,), (1,)))
        own = lax.dynamic_slice_in_dim(diag_inverse[k], own_first, local_rows, 1).T
        tops = [jnp.zeros((local_rows, width), jnp.float32) for _ in range(PANELS)]
        tops[k] = -own
        left.append(jnp.concatenate(tops + [part], axis=0))
    u10 = dot(c10, slots[0], ((1,), (1,)))
    u20 = dot(c20, slots[0], ((1,), (1,)))
    u21 = dot(c21, slots[1], ((1,), (1,)))
    m2 = left[2]
    m1 = left[1] - dot(m2, u21, ((1,), (0,)))
    m0 = left[0] - dot(m2, u20, ((1,), (0,))) - dot(m1, u10, ((1,), (0,)))
    m = jnp.concatenate([m0, m1, m2], axis=1)
    product = dot(m, panels.reshape(PANELS * width, columns), ((1,), (0,)))
    base = jnp.where(jnp.arange(cycles)[:, None, None] < PANELS, 0.0, grad_t)
    return base - product.reshape(grad_t.shape)


def solution(mesh):
    in_specs = (P(None, "col", "row"), P(None, "col", None, "row"), P())
    out_specs = P(None, "col", "row")
    rows, cols = mesh.shape["row"], mesh.shape["col"]

    def step(*args):
        return body(rows, cols, *args)

    return jax.shard_map(step, mesh=mesh, in_specs=in_specs, out_specs=out_specs, check_vma=False)
```
